32 devices in a mesh: grp: 4 (over y, x), wide: 8 (over z, core).
Axes of the slice: x: 2, y: 2, z: 4, core: 2. Of those that a mesh axis runs over, the one named last changes fastest.
Arguments:
- spectral: float32 [8, 48, 320, 2, 641], P(None, 'grp', 'wide'), may hold values from -0.006 to 0.006
- legendre: float32 [320, 641, 320], P('wide'), may hold values from -18 to 18
- pair_table: int32 [320], replicated, may hold values from 0 to 319, each once
- field_map: int32 [8], replicated, may hold values from 0 to 7, each once
Outputs:
- grid_values: float32 [8, 48, 640, 1280], P('grp', None, 'wide')
- checksums: float32 [8, 48], replicated
The draws below stay inside these ranges and needn't reach their ends.
Inputs may be any that keep to these rules, and one draw needn't show every extreme that they name: Each slot number appears once; slot s holds wavenumbers pair_table[s] and 639 - pair_table[s]. `field_map`: each field appears once.
All inputs are finite; a program needn't handle non-finite values.
Results may differ from the reference program's by a relative error of at most 0.000078.
Values sent between devices are 32-bit elements; how exact they have to be, the bound alone decides.
No kernel may reach another device: no remote copies, remote signals or barrier semaphores. Data moves between devices by JAX's collectives and lax.ppermute only.
A program may use at most 448 MiB of HBM per device.

```python
import math
import jax
import jax.numpy as jnp
from jax import lax

WAVES = 640
LAT = 640
LON = 1280
FIELDS = 8
LEVELS = 48
PAIRS = 320
NPAIR = 641


def draw_legendre(key, part):
    base_key = jax.random.fold_in(key, 11)
    row_key = jax.random.fold_in(key, 12)
    dimensions = (WAVES // 2, WAVES + 1, LAT // 2)
    values = jnp.clip(jax.random.normal(base_key, dimensions, jnp.float32), -6.0, 6.0)
    scales = jnp.exp(jax.random.uniform(row_key, (LAT // 2,), jnp.float32, math.log(0.3), math.log(3.0)))
    return values * scales


def shard_levels(stream_key, dims, shards, smallest, high):
    loudness, own = 1.0, jax.random.fold_in(stream_key, 6)
    for dim, shards_of in shards:
        heights = jnp.exp(jax.random.uniform(jax.random.fold_in(own, dim), (shards_of,), jnp.float32, smallest / len(shards), high / len(shards)))
        loudness = loudness * jnp.repeat(heights, dims[dim] // shards_of).reshape([-1 if axis == dim else 1 for axis in range(len(dims))])
    return loudness


def gaussian(key, dims, deviation, bound, shards=(), kind=jnp.bfloat16):
    values = jax.random.normal(key, dims, jnp.float32) * deviation
    if len(shards) > 0:
        values = shard_levels(key, dims, shards, -0.22, 0.18) * values
    return jnp.clip(values, min=-bound, max=bound).astype(kind)


def setup_inputs(seed: int = 0) -> dict:
    streams_of = jax.random.split(jax.random.key(seed), 5)
    return {
        "spectral": gaussian(streams_of[0], (FIELDS, LEVELS, PAIRS, 2, NPAIR), 0.001, 0.006, ((1, 4), (2, 8)), jnp.float32),
        "legendre": draw_legendre(jax.random.fold_in(streams_of[4], 71), 0),
        "pair_table": jax.random.permutation(streams_of[2], PAIRS).astype(jnp.int32),
        "field_map": jax.random.permutation(streams_of[3], FIELDS).astype(jnp.int32),
    }


HIGHEST = lax.Precision.HIGHEST


def parity_masks(slot_pairs):
    degree = jnp.arange(WAVES + 1, dtype=jnp.int32)[None, :]
    boundary = (WAVES - slot_pairs.astype(jnp.int32))[:, None]
    first_part = degree < boundary
    first_even = (degree % 2) == 0
    second_even = ((degree - boundary) % 2) == 0
    stacked = jnp.stack([first_part & first_even, first_part & ~first_even,
                         ~first_part & second_even, ~first_part & ~second_even], 0)
    return stacked.astype(jnp.float32)


def legendre_sums(coeffs, legendre, slot_pairs):
    weights = parity_masks(slot_pairs)
    masked = coeffs[None] * weights[:, None, None, :, None, :]
    summed = jnp.einsum('qflprk,pkh->pqrflh', masked, legendre, precision=HIGHEST)
    even_sums = summed[:, 0::2]
    odd_sums = summed[:, 1::2]
    return jnp.concatenate([even_sums + odd_sums, jnp.flip(even_sums - odd_sums, -1)], -1)


def reference(spectral, legendre, pair_table, field_map):
    ordered = jnp.take(spectral, field_map.astype(jnp.int32), axis=0)
    wavenumber = jnp.stack([pair_table, WAVES - 1 - pair_table], 1).reshape(-1).astype(jnp.int32)

    def one_field(coeffs):
        fourier = legendre_sums(coeffs[None], legendre, pair_table)[:, :, :, 0]
        real_part = jnp.moveaxis(fourier[:, :, 0].reshape(-1, LEVELS, LAT), 0, -1)
        imag_part = jnp.moveaxis(fourier[:, :, 1].reshape(-1, LEVELS, LAT), 0, -1)
        spectrum_real = jnp.zeros((LEVELS, LAT, LON // 2 + 1), jnp.float32).at[:, :, wavenumber].set(real_part)
        spectrum_imag = jnp.zeros((LEVELS, LAT, LON // 2 + 1), jnp.float32).at[:, :, wavenumber].set(imag_part)
        spectrum_imag = spectrum_imag.at[:, :, 0].set(0.0)
        return LON * jnp.fft.irfft(spectrum_real + 1j * spectrum_imag, n=LON, axis=-1)

    grid_values = lax.map(one_field, ordered).astype(jnp.float32)
    checksums = jnp.mean(grid_values * grid_values, axis=(2, 3))
    return grid_values, checksums
```

```python
import math

import jax
import jax.numpy as jnp
from jax import lax
from jax.sharding import PartitionSpec as P

WAVES = 640
LAT = 640
LON = 1280


HIGH = lax.Precision.HIGH
MOST_CHUNKS = 4


def coefficient_weights(slot_pairs, coeff_count):
    degree = jnp.arange(coeff_count, dtype=jnp.int32)[None, :]
    boundary = (WAVES - slot_pairs)[:, None]
    first_part = degree < boundary
    within = jnp.where(first_part, degree, degree - boundary)
    sign = jnp.where(within % 2 == 0, 1.0, -1.0).astype(jnp.float32)
    pair_even = (slot_pairs % 2 == 0)[:, None]
    even_wave = (first_part == pair_even).astype(jnp.float32)
    belong = jnp.stack([even_wave, 1.0 - even_wave], 1)
    return belong, belong * sign[:, None, :]


def legendre_sums(coeffs, weights, legendre):
    by_slot = jnp.transpose(coeffs, (2, 3, 0, 1, 4))
    masked = weights[:, :, None, None, None, :] * by_slot[:, None]
    slots, _, _, _, _, depth = masked.shape
    masked = masked.reshape(slots, -1, depth)
    return lax.dot_general(
        legendre,
        masked,
        (((1,), (2,)), ((0,), (0,))),
        precision=HIGH,
        preferred_element_type=jnp.float32,
    )


def synthesis_table(pairs):
    other = WAVES - 1 - pairs
    even = pairs % 2 == 0
    numbers = jnp.stack([jnp.where(even, pairs, other), jnp.where(even, other, pairs)], 0)
    columns = jnp.arange(LON // 2, dtype=jnp.int32)
    phases = numbers[:, :, None] * columns % LON
    angles = phases.astype(jnp.float32) * (2.0 * math.pi / LON)
    factor = jnp.where(numbers == 0, 1.0, 2.0).astype(jnp.float32)[:, :, None]
    return jnp.stack([factor * jnp.cos(angles), -factor * jnp.sin(angles)], 2)


def local(spectral, legendre, pair_table, field_map):
    slot_count = legendre.shape[0]
    coeff_count = legendre.shape[1]
    wide = lax.axis_size("wide")
    chunks = max(n for n in range(1, MOST_CHUNKS + 1) if slot_count % n == 0)
    size = slot_count // chunks
    own_pairs = lax.dynamic_slice_in_dim(
        pair_table, lax.axis_index("wide") * slot_count, slot_count
    )
    north_weights, south_weights = coefficient_weights(own_pairs, coeff_count)
    fields = None
    levels = None
    arrived = []
    for chunk in range(chunks):
        start, stop = chunk * size, (chunk + 1) * size
        part = jnp.take(spectral[:, :, start:stop], field_map, axis=0)
        part = lax.all_to_all(part, "grp", split_axis=0, concat_axis=1, tiled=True)
        fields, levels = part.shape[0], part.shape[1]
        table = legendre[start:stop]
        north = legendre_sums(part, north_weights[start:stop], table)
        south = legendre_sums(part, south_weights[start:stop], jnp.flip(table, -1))
        fourier = jnp.concatenate([north, south], 1)
        arrived.append(
            lax.all_to_all(fourier, "wide", split_axis=1, concat_axis=0, tiled=True)
        )
    collected = jnp.concatenate(arrived, 0)
    slots, band = collected.shape[0], collected.shape[1]
    collected = collected.reshape(slots, band, 2, 2, fields, levels)
    ordered_pairs = pair_table.reshape(wide, chunks, size).transpose(1, 0, 2).reshape(-1)
    synthesis = synthesis_table(ordered_pairs)
    halves = [
        lax.dot_general(
            collected[:, :, parity],
            synthesis[parity],
            (((0, 2), (0, 1)), ((), ())),
            precision=HIGH,
            preferred_element_type=jnp.float32,
        )
        for parity in range(2)
    ]
    even, odd = [jnp.transpose(half, (1, 2, 0, 3)) for half in halves]
    gridded = jnp.concatenate([even + odd, even - odd], -1)
    local_sum = 2.0 * jnp.sum(even * even + odd * odd, axis=(2, 3))
    summed = lax.psum(local_sum, "wide")
    checksums = lax.all_gather(summed, "grp", axis=0, tiled=True) / (LAT * LON)
    return (gridded, checksums)


def solution(mesh):
    placed = (P(None, "grp", "wide", None, None), P("wide", None, None), P(), P())
    return jax.shard_map(
        local,
        mesh=mesh,
        in_specs=placed,
        out_specs=(P("grp", None, "wide", None), P()),
        check_vma=False,
    )
```
